32 devices in a mesh: gx: 4 (over y, x), gy: 2 (over core), gz: 4 (over z).
Axes of the slice: x: 2, y: 2, z: 4, core: 2. Of those that a mesh axis runs over, the one named last changes fastest.
Arguments:
- density: bfloat16 [4, 2, 4, 512, 256], P('gx', 'gy', 'gz'), may hold values from -6 to 6
- integrals: bfloat16 [4, 2, 4, 9, 512, 512], P('gx', 'gy', 'gz'), may hold values from -0.25 to 0.25
- offsets: int32 [4, 2, 4, 9], P('gx', 'gy', 'gz'), may hold values from 0 to 26, as said below
- counts: int32 [4, 2, 4], P('gx', 'gy', 'gz'), may hold values from 7 to 9, as said below
Outputs:
- exchange: bfloat16 [4, 2, 4, 512, 256], P('gx', 'gy', 'gz')
The draws below stay inside these ranges and needn't reach their ends.
Inputs may be any that keep to these rules, and one draw needn't show every extreme that they name: Slots from counts[p] on hold no tile of domain p; some domain has all 9 slots live in every draw. `offsets`: a code names one of the 27 domains within one step along each axis, as the steps say; the 9 codes of one domain are all different.
All inputs are finite; a program needn't handle non-finite values.
Results may differ from the reference program's by a relative error of at most 0.006.
Values may be sent and summed in bfloat16 or wider, within the bound.
No kernel may reach another device: no remote copies, remote signals or barrier semaphores. Data moves between devices by JAX's collectives and lax.ppermute only.
A program may use at most 64 MiB of HBM per device.

```python
import jax
import jax.numpy as jnp
from jax import lax

BLK = 512
NCOL = 256
TCAP = 9
DX = 4
DY = 2
DZ = 4


def draw_counts(key, part):
    key_one = jax.random.fold_in(key, 11)
    key_three = jax.random.fold_in(key, 13)
    shape_all = (DX, DY, DZ)
    missing = jax.random.randint(key_one, shape_all, 0, (TCAP + 2) // 3)
    loads = TCAP - missing
    loads_flat = loads.reshape(-1)
    busiest = jax.random.randint(key_three, (), 0, DX * DY * DZ)
    loads_flat = loads_flat.at[busiest].set(TCAP)
    return loads_flat.reshape(shape_all).astype(jnp.int32)


def draw_offsets(key, part):
    key_perm = jax.random.fold_in(key, 21)
    domain_keys = jax.random.split(key_perm, DX * DY * DZ)
    rows = jax.vmap(lambda single: jax.random.permutation(single, 27)[:TCAP])(domain_keys)
    return rows.reshape(DX, DY, DZ, TCAP).astype(jnp.int32)


def levels(own_key, dims, cuts, smallest, top_value):
    level = 1.0
    for position, shards_of in cuts:
        draws = jax.random.uniform(jax.random.fold_in(jax.random.fold_in(own_key, 6), position), (shards_of,), jnp.float32, smallest / len(cuts), top_value / len(cuts))
        level = level * jnp.repeat(jnp.exp(draws), dims[position] // shards_of).reshape((-1,) + (1,) * (len(dims) - 1 - position))
    return level


def gaussian(rng, extent, deviation, limit, cuts=(), held_as=jnp.bfloat16):
    loudness = levels(rng, extent, cuts, -0.22, 0.18) if cuts else 1.0
    values = jax.random.normal(rng, extent, jnp.float32) * deviation * loudness
    return jnp.minimum(jnp.maximum(values, -limit), limit).astype(held_as)


def setup_inputs(seed: int = 0) -> dict:
    seeds = jax.random.split(jax.random.key(seed), 5)
    return {
        "density": gaussian(seeds[0], (DX, DY, DZ, BLK, NCOL), 1.0, 6.0, ((0, 4), (1, 2), (2, 4))),
        "integrals": gaussian(seeds[1], (DX, DY, DZ, TCAP, BLK, BLK), BLK ** -0.5, 0.25, ((0, 4), (1, 2), (2, 4))),
        "offsets": draw_offsets(jax.random.fold_in(seeds[4], 71), 0),
        "counts": draw_counts(jax.random.fold_in(seeds[4], 71), 0),
    }


def reference(density, integrals, offsets, counts):
    extent_x, extent_y, extent_z = density.shape[0], density.shape[1], density.shape[2]
    block_rows = density.shape[3]
    columns = density.shape[4]
    slot_total = integrals.shape[3]
    domains = extent_x * extent_y * extent_z
    dens_flat = density.reshape(domains, block_rows, columns)
    tile_flat = integrals.reshape(domains, slot_total, block_rows, block_rows)
    code_flat = offsets.reshape(domains, slot_total).astype(jnp.int32)
    live_flat = counts.reshape(domains).astype(jnp.int32)
    domain_ids = jnp.arange(domains, dtype=jnp.int32)
    coord_x = domain_ids // (extent_y * extent_z)
    coord_y = (domain_ids // extent_z) % extent_y
    coord_z = domain_ids % extent_z
    step_x = code_flat // 9 - 1
    step_y = (code_flat // 3) % 3 - 1
    step_z = code_flat % 3 - 1
    neighbour = (((coord_x[:, None] + step_x) % extent_x) * extent_y + (coord_y[:, None] + step_y) % extent_y) * extent_z + (coord_z[:, None] + step_z) % extent_z
    neighbour = neighbour.astype(jnp.int32)

    def visit_domain(total, item):
        tile_block, nbr_ids, live_count, home_index = item
        slot_live = (jnp.arange(slot_total, dtype=jnp.int32) < live_count).astype(jnp.float32)
        blocks = dens_flat[nbr_ids].astype(jnp.float32)
        tile_wide = tile_block.astype(jnp.float32) * slot_live[:, None, None]
        forward = jnp.einsum('sij,sjc->ic', tile_wide, blocks, precision=lax.Precision.HIGHEST)
        own_block = dens_flat[home_index].astype(jnp.float32)
        partial_value = jnp.einsum('sji,jc->sic', tile_wide, own_block, precision=lax.Precision.HIGHEST)
        partial_value = lax.optimization_barrier(partial_value.astype(jnp.bfloat16)).astype(jnp.float32)
        total = total.at[home_index].add(forward)
        total = total.at[nbr_ids].add(partial_value)
        return total, None

    start = jnp.zeros((domains, block_rows, columns), jnp.float32)
    total, _ = lax.scan(visit_domain, start, (tile_flat, neighbour, live_flat, domain_ids))
    return total.astype(jnp.bfloat16).reshape(density.shape)
```

```python
import functools

import jax
import jax.numpy as jnp
from jax import lax
from jax.experimental import pallas as pl
from jax.experimental.pallas import tpu as pltpu
from jax.sharding import PartitionSpec as P


F32 = jnp.float32
BF16 = jnp.bfloat16


class Axis:
    def __init__(self, name, size, paired):
        self.name = name
        self.size = size
        self.paired = paired and size >= 4 and size % 2 == 0
        self.classes = min(size, 3)

    def pairs(self, cls):
        out = []
        for i in range(self.size):
            if not self.paired:
                step = 1 if cls == 1 else -1
            else:
                step = 1 if (cls == 1) == (i % 2 == 0) else -1
            out.append((i, (i + step) % self.size))
        return out

    def to(self, block, cls):
        return lax.ppermute(block, self.name, self.pairs(cls))

    def of(self, block, cls):
        return lax.ppermute(block, self.name, [(t, s) for s, t in self.pairs(cls)])

    def hop(self, block):
        half = self.size // 2
        return lax.ppermute(block, self.name, [(i, (i + half) % self.size) for i in range(self.size)])

    @property
    def relay(self):
        return self.paired and self.size == 4

    def class_of(self, step):
        if self.classes == 1:
            return step * 0
        if self.classes == 2:
            return jnp.where(step == 0, 0, 1)
        if self.paired:
            up = 1 - 2 * lax.rem(lax.axis_index(self.name), 2)
        else:
            up = 1
        return jnp.where(step == 0, 0, jnp.where(step == up, 1, 2))


def slot_classes(axes, code):
    ax, ay, az = axes
    return (
        ax.class_of(lax.div(code, 9) - 1),
        ay.class_of(lax.rem(lax.div(code, 3), 3) - 1),
        az.class_of(lax.rem(code, 3) - 1),
    )


def partial_kernel(axes, off_ref, cnt_ref, d_ref, t_ref, *rest):
    ax, ay, az = axes
    outs, (dt_ref, val_ref) = rest[:-2], rest[-2:]
    for out in outs:
        out[...] = jnp.zeros_like(out)
    dt_ref[...] = d_ref[...].T

    def body(s, carry):
        cx, cy, cz = slot_classes(axes, off_ref[s])
        val_ref[...] = jnp.dot(dt_ref[...], t_ref[s], preferred_element_type=F32)
        where = (cy * ax.classes + cx) * az.classes + cz
        for k, out in enumerate(outs):
            blocks = out.shape[0]
            local = where - k * blocks

            @pl.when((local >= 0) & (local < blocks))
            def _():
                out[local] = (out[local].astype(F32) + val_ref[...]).astype(BF16)

        return carry

    lax.fori_loop(0, cnt_ref[0], body, 0)


def forward_kernel(axes, groups, last, off_ref, cnt_ref, t_ref, *rest):
    ax, ay, az = axes
    n = len(groups)
    blocks, rest = rest[:n], rest[n:]
    if last:
        acc_in, inc_refs, out_ref, acc, sel = rest[0], rest[1:-3], rest[-3], rest[-2], rest[-1]
        acc[...] = acc_in[...]
    else:
        acc, sel = rest
        acc[...] = jnp.zeros_like(acc)

    def body(s, carry):
        cx, cy, cz = slot_classes(axes, off_ref[s])
        where = (cy * ax.classes + cx) * az.classes + cz
        found = where < 0
        for (gy, gx, gz), ref in zip(groups, blocks):
            here = where == (gy * ax.classes + gx) * az.classes + gz
            found = found | here

            @pl.when(here)
            def _():
                sel[...] = ref[...]

        @pl.when(found)
        def _():
            acc[...] += jnp.dot(t_ref[s], sel[...], preferred_element_type=F32)

        return carry

    lax.fori_loop(0, cnt_ref[0], body, 0)
    if last:
        total = inc_refs[0][...].astype(F32)
        for ref in inc_refs[1:]:
            total += ref[...].astype(F32)
        out_ref[...] = (acc[...] + total.T).astype(BF16)


VMEM = pl.BlockSpec(memory_space=pltpu.VMEM)
SMEM = pl.BlockSpec(memory_space=pltpu.SMEM)


def add(*blocks):
    total = blocks[0].astype(F32)
    for block in blocks[1:]:
        total = total + block.astype(F32)
    return total.astype(BF16)


def local(axes, density, integrals, offsets, counts):
    ax, ay, az = axes
    rows, cols = density.shape[3:]
    slots = integrals.shape[3]
    own = density.reshape(rows, cols)
    tiles = integrals.reshape(slots, rows, rows)
    codes = offsets.reshape(slots)
    live = counts.reshape(1)
    nx, ny, nz = ax.classes, ay.classes, az.classes

    flops = 2 * slots * rows * rows * cols
    parts = pl.pallas_call(
        functools.partial(partial_kernel, axes),
        out_shape=[jax.ShapeDtypeStruct((nz, cols, rows), BF16)] * (ny * nx),
        in_specs=[SMEM, SMEM, VMEM, VMEM],
        out_specs=[VMEM] * (ny * nx),
        scratch_shapes=[pltpu.VMEM((cols, rows), BF16), pltpu.VMEM((cols, rows), F32)],
        cost_estimate=pl.CostEstimate(flops=flops, transcendentals=0, bytes_accessed=tiles.size * 2),
        name="partials",
    )(codes, live, own, tiles)
    part = lambda cy, cx: parts[cy * nx + cx]

    got = {(0, 0, 0): own}
    for cz in range(1, nz):
        got[0, 0, cz] = az.of(own, cz)
    for cz in range(nz):
        for cx in range(1, nx):
            if cx == 2 and ax.relay:
                got[0, 2, cz] = ax.hop(got[0, 1, cz])
            else:
                got[0, cx, cz] = ax.of(got[0, 0, cz], cx)
    for cx in range(nx):
        stack = jnp.stack([got[0, cx, cz] for cz in range(nz)])
        for cy in range(1, ny):
            brought = ay.of(stack, cy)
            for cz in range(nz):
                got[cy, cx, cz] = brought[cz]

    mine = {}
    for cx in reversed(range(nx)):
        summed = add(part(0, cx), *[ay.to(part(cy, cx), cy) for cy in range(1, ny)])
        for cz in range(nz):
            mine[cx, cz] = summed[cz]
    order = list(range(1, nz)) + [0]
    for cz in order:
        if ax.relay:
            mine[1, cz] = add(mine[1, cz], ax.hop(mine[2, cz]))
            mine[0, cz] = add(mine[0, cz], ax.to(mine[1, cz], 1))
        else:
            mine[0, cz] = add(mine[0, cz], *[ax.to(mine[cx, cz], cx) for cx in range(1, nx)])
    incoming = [mine[0, 0]] + [az.to(mine[0, cz], cz) for cz in range(1, nz)]

    def forward(groups, last, *extra):
        return pl.pallas_call(
            functools.partial(forward_kernel, axes, groups, last),
            out_shape=jax.ShapeDtypeStruct((rows, cols), BF16 if last else F32),
            in_specs=[SMEM, SMEM, VMEM] + [VMEM] * (len(groups) + len(extra)),
            out_specs=VMEM,
            scratch_shapes=([pltpu.VMEM((rows, cols), F32)] if last else []) + [pltpu.VMEM((rows, cols), BF16)],
            cost_estimate=pl.CostEstimate(flops=flops // 2, transcendentals=0, bytes_accessed=tiles.size),
            name="forward_last" if last else "forward",
        )(codes, live, tiles, *[got[g] for g in groups], *extra)

    keys = [(cy, cx, cz) for cx in range(nx) for cy in range(ny) for cz in range(nz)]
    early = tuple(k for k in keys if k[1] < nx - 1)
    late = tuple(k for k in keys if k[1] == nx - 1)
    if not early:
        early, late = late[:1], late[1:]
    acc = forward(early, False)
    out = forward(late, True, acc, *incoming)
    return out.reshape(density.shape)


def solution(mesh):
    axes = (
        Axis("gx", mesh.shape["gx"], True),
        Axis("gy", mesh.shape["gy"], False),
        Axis("gz", mesh.shape["gz"], False),
    )
    return jax.shard_map(
        functools.partial(local, axes),
        mesh=mesh,
        in_specs=(
            P("gx", "gy", "gz", None, None),
            P("gx", "gy", "gz", None, None, None),
            P("gx", "gy", "gz", None),
            P("gx", "gy", "gz"),
        ),
        out_specs=P("gx", "gy", "gz", None, None),
        check_vma=False,
    )
```
